32 devices in a mesh: blk: 8 (over y, x, core), uly: 4 (over z).
Axes of the slice: x: 2, y: 2, z: 4, core: 2. Of those that a mesh axis runs over, the one named last changes fastest.
Arguments:
- tokens: bfloat16 [4096, 2048], P(('blk', 'uly')), may hold values from -6 to 6
- doc_starts: int32 [16], replicated, may hold values from 0 to 4095, as said below
- attn_gain: bfloat16 [2048], P(('blk', 'uly')), may hold values from 0.25 to 1.75
- qk_gains: bfloat16 [128], P(('blk', 'uly')), may hold values from 0.25 to 1.75
- q_weight: bfloat16 [2048, 2048], P(('blk', 'uly')), may hold values from -0.125 to 0.125
- k_weight: bfloat16 [512, 2048], P(('blk', 'uly')), may hold values from -0.125 to 0.125
- v_weight: bfloat16 [512, 2048], P(('blk', 'uly')), may hold values from -0.125 to 0.125
- out_weight: bfloat16 [2048, 2048], P(('blk', 'uly')), may hold values from -1 to 1
- ffn_gain: bfloat16 [2048], P(('blk', 'uly')), may hold values from 0.25 to 1.75
- gate_weight: bfloat16 [8192, 2048], P(('blk', 'uly')), may hold values from -0.125 to 0.125
- up_weight: bfloat16 [8192, 2048], P(('blk', 'uly')), may hold values from -0.125 to 0.125
- down_weight: bfloat16 [8192, 2048], P(('blk', 'uly')), may hold values from -0.0625 to 0.0625
- out_grad: bfloat16 [4096, 2048], P(('blk', 'uly')), may hold values from -6 to 6
Outputs:
- output: float32 [4096, 2048], P(('blk', 'uly'))
- input_grad: float32 [4096, 2048], P(('blk', 'uly'))
- attn_gain_grad: float32 [2048], P(('blk', 'uly'))
- qk_gains_grad: float32 [128], P(('blk', 'uly'))
- q_weight_grad: float32 [2048, 2048], P(('blk', 'uly'))
- k_weight_grad: float32 [512, 2048], P(('blk', 'uly'))
- v_weight_grad: float32 [512, 2048], P(('blk', 'uly'))
- out_weight_grad: float32 [2048, 2048], P(('blk', 'uly'))
- ffn_gain_grad: float32 [2048], P(('blk', 'uly'))
- gate_weight_grad: float32 [8192, 2048], P(('blk', 'uly'))
- up_weight_grad: float32 [8192, 2048], P(('blk', 'uly'))
- down_weight_grad: float32 [8192, 2048], P(('blk', 'uly'))
The draws below stay inside these ranges and needn't reach their ends.
Inputs may be any that keep to these rules, and one draw needn't show every extreme that they name: doc_starts[0] = 0 and the starts rise strictly; a document runs from its start to the next start, the last one to 4096; every document holds at most 2048 tokens, and one holds exactly 2048.
All inputs are finite; a program needn't handle non-finite values.
Results may differ from the reference program's by a relative error of at most 0.03.
Values may be sent and summed in bfloat16 or wider, within the bound.
A program may use at most 256 MiB of HBM per device.

```python
from functools import partial
import jax
import jax.numpy as jnp
from jax import lax

D = 2048
H = 32
KVH = 8
HD = 64
FF = 8192
DOC_MAX = 2048
TOKENS = 4096
LONGEST = 2048
NDOC = 16


def draw_doc_starts(key, part):
    longest = min(DOC_MAX, TOKENS // 2)
    remaining = TOKENS - longest
    pieces = NDOC - 1
    jitter = max(remaining // (2 * pieces) - 1, 0)
    key_cut = jax.random.fold_in(key, 11)
    key_long = jax.random.fold_in(key, 12)
    inner_cuts = jnp.arange(1, pieces, dtype=jnp.int32)
    even_cuts = inner_cuts * remaining // pieces
    offsets = jax.random.randint(key_cut, (pieces - 1,), -jitter, jitter + 1, dtype=jnp.int32)
    cut_points = jnp.concatenate([jnp.zeros((1,), jnp.int32), even_cuts + offsets, jnp.full((1,), remaining, jnp.int32)])
    long_index = jax.random.randint(key_long, (), 1, pieces, dtype=jnp.int32)
    doc_index = jnp.arange(NDOC, dtype=jnp.int32)
    early_start = cut_points[jnp.minimum(doc_index, pieces)]
    late_start = cut_points[jnp.maximum(doc_index - 1, 0)] + longest
    return jnp.where(doc_index <= long_index, early_start, late_start).astype(jnp.int32)


def level_of(stream_key, shape, split, low, largest):
    loudness, own = 1.0, jax.random.fold_in(stream_key, 6)
    for dim, blocks in split:
        steps = jnp.exp(jax.random.uniform(jax.random.fold_in(own, dim), (blocks,), jnp.float32, low / len(split), largest / len(split)))
        loudness = loudness * jnp.repeat(steps, shape[dim] // blocks).reshape([-1 if axis == dim else 1 for axis in range(len(shape))])
    return loudness


def gaussian(key, extent, width, reach, cuts=(), kind=jnp.bfloat16):
    drawn = jax.random.normal(key, extent, jnp.float32) * width
    if len(cuts) > 0:
        drawn = level_of(key, extent, cuts, -0.22, 0.18) * drawn
    return jnp.clip(drawn, min=-reach, max=reach).astype(kind)


def setup_inputs(seed: int = 0) -> dict:
    key_of = jax.random.split(jax.random.key(seed), 14)
    tokens = gaussian(key_of[0], (TOKENS, D), 1.0, 6.0, ((0, 32),))
    doc_starts = draw_doc_starts(jax.random.fold_in(key_of[13], 71), 0)
    attn_gain = jnp.clip(1.0 + 0.15 * jax.random.normal(key_of[2], (D,), jnp.float32), 0.25, 1.75).astype(jnp.bfloat16)
    qk_gains = jnp.clip(1.0 + 0.15 * jax.random.normal(key_of[3], (2 * HD,), jnp.float32), 0.25, 1.75).astype(jnp.bfloat16)
    q_weight = gaussian(key_of[4], (H * HD, D), D ** -0.5, 0.125, ((0, 32),))
    k_weight = gaussian(key_of[5], (KVH * HD, D), D ** -0.5, 0.125, ((0, 32),))
    v_weight = gaussian(key_of[6], (KVH * HD, D), D ** -0.5, 0.125, ((0, 32),))
    out_weight = gaussian(key_of[7], (D, H * HD), (H * HD // 64) ** -0.5, 1.0, ((0, 32),))
    ffn_gain = jnp.clip(1.0 + 0.15 * jax.random.normal(key_of[8], (D,), jnp.float32), 0.25, 1.75).astype(jnp.bfloat16)
    gate_weight = gaussian(key_of[9], (FF, D), D ** -0.5, 0.125, ((0, 32),))
    up_weight = gaussian(key_of[10], (FF, D), D ** -0.5, 0.125, ((0, 32),))
    down_weight = gaussian(key_of[11], (FF, D), FF ** -0.5, 0.0625, ((0, 32),))
    out_grad = gaussian(key_of[12], (TOKENS, D), 1.0, 6.0, ((0, 32),))
    return {"tokens": tokens, "doc_starts": doc_starts, "attn_gain": attn_gain, "qk_gains": qk_gains, "q_weight": q_weight, "k_weight": k_weight, "v_weight": v_weight, "out_weight": out_weight, "ffn_gain": ffn_gain, "gate_weight": gate_weight, "up_weight": up_weight, "down_weight": down_weight, "out_grad": out_grad}


@jax.custom_vjp
def low(v):
    return lax.optimization_barrier(v.astype(jnp.bfloat16)).astype(jnp.float32)

@jax.custom_vjp
def low_back(v):
    return v

def low_keep(v):
    return (low(v), None)

def low_pass(kept, grad):
    return (grad,)

def back_keep(v):
    return (v, None)

def back_low(kept, grad):
    return (low(grad),)
low.defvjp(low_keep, low_pass)
low_back.defvjp(back_keep, back_low)
NORM_EPSILON = 1e-05
ROPE_THETA = 1000000.0
MASKED_SCORE = -1e+30
FULL_PRECISION = lax.Precision.HIGHEST

def rms_scale(values, gain):
    inverse = lax.rsqrt(lax.optimization_barrier(jnp.mean(values * values, axis=-1, keepdims=True)) + NORM_EPSILON)
    return values * inverse * gain

def rotate(values, cosine, sine):
    half_width = values.shape[-1] // 2
    front_half = values[..., :half_width]
    back_half = values[..., half_width:]
    return jnp.concatenate([front_half * cosine - back_half * sine, back_half * cosine + front_half * sine], axis=-1)

def project(inputs, weight):
    return jnp.dot(inputs, weight.T, precision=FULL_PRECISION)

def forward(cosine, sine, doc_start, hidden_in, attn_gain, qk_gains, q_weight, k_weight, v_weight, out_weight, ffn_gain, gate_weight, up_weight, down_weight):
    token_count = hidden_in.shape[0]
    normed_one = low(rms_scale(hidden_in, attn_gain))
    q_raw = low_back(project(normed_one, q_weight))
    k_raw = low_back(project(normed_one, k_weight))
    v_raw = low_back(project(normed_one, v_weight))
    q_heads = rotate(rms_scale(q_raw.reshape(token_count, H, HD), qk_gains[:HD]), cosine, sine)
    k_heads = rotate(rms_scale(k_raw.reshape(token_count, KVH, HD), qk_gains[HD:]), cosine, sine)
    queries = low(q_heads).reshape(token_count, KVH, H // KVH, HD)
    key_heads = low(k_heads)
    value_heads = low(v_raw).reshape(token_count, KVH, HD)
    block_rows = min(512, token_count)
    window = min(LONGEST + block_rows, token_count)
    score_scale = HD ** (-0.5)

    def attend(block_start):
        key_start = jnp.clip(block_start - LONGEST, 0, token_count - window).astype(jnp.int32)
        query_block = lax.dynamic_slice_in_dim(queries, block_start, block_rows, 0)
        key_block = lax.dynamic_slice_in_dim(key_heads, key_start, window, 0)
        value_block = lax.dynamic_slice_in_dim(value_heads, key_start, window, 0)
        query_doc = lax.dynamic_slice_in_dim(doc_start, block_start, block_rows, 0)
        query_rows = block_start + jnp.arange(block_rows, dtype=jnp.int32)
        key_rows = key_start + jnp.arange(window, dtype=jnp.int32)
        raw_scores = jnp.einsum('qkgd,skd->qkgs', query_block, key_block, precision=FULL_PRECISION)
        scores = low_back(raw_scores * score_scale)
        allowed = (key_rows[None, :] >= query_doc[:, None]) & (key_rows[None, :] <= query_rows[:, None])
        scores = jnp.where(allowed[:, None, None, :], scores, MASKED_SCORE)
        weights = low(jax.nn.softmax(scores, axis=-1))
        mixed = jnp.einsum('qkgs,skd->qkgd', weights, value_block, precision=FULL_PRECISION)
        return mixed.reshape(block_rows, H * HD)
    attended = lax.map(jax.checkpoint(attend), jnp.arange(0, token_count, block_rows, dtype=jnp.int32))
    attended = low(low_back(attended.reshape(token_count, H * HD)))
    hidden = hidden_in + low_back(project(attended, out_weight))
    normed_two = low(rms_scale(hidden, ffn_gain))
    gate = low_back(project(normed_two, gate_weight))
    upward = low_back(project(normed_two, up_weight))
    active = low(jax.nn.silu(gate) * upward)
    return hidden + low_back(jnp.dot(active, down_weight, precision=FULL_PRECISION))

def reference(tokens, doc_starts, attn_gain, qk_gains, q_weight, k_weight, v_weight, out_weight, ffn_gain, gate_weight, up_weight, down_weight, out_grad):
    row_ids = jnp.arange(TOKENS, dtype=jnp.int32)
    doc_start = lax.optimization_barrier(jnp.max(jnp.where(doc_starts[None, :] <= row_ids[:, None], doc_starts[None, :], 0), axis=1)).astype(jnp.int32)
    positions = (row_ids - doc_start).astype(jnp.float32)
    frequency = ROPE_THETA ** (-jnp.arange(HD // 2, dtype=jnp.float32) * 2.0 / HD)
    angle = positions[:, None] * frequency[None, :]
    cosine = jnp.cos(angle)[:, None, :]
    sine = jnp.sin(angle)[:, None, :]
    primals = tuple((array_in.astype(jnp.float32) for array_in in (tokens, attn_gain, qk_gains, q_weight, k_weight, v_weight, out_weight, ffn_gain, gate_weight, up_weight, down_weight)))
    output, pullback = jax.vjp(partial(forward, cosine, sine, doc_start), *primals)
    grads = pullback(out_grad.astype(jnp.float32))
    return (output, grads[0], grads[1], grads[2], grads[3], grads[4], grads[5], grads[6], grads[7], grads[8], grads[9], grads[10])
```

```python
import functools

import jax
import jax.numpy as jnp
from jax import lax
from jax.experimental import pallas as pl
from jax.experimental.pallas import tpu as pltpu
from jax.sharding import Mesh
from jax.sharding import PartitionSpec as P

H = 32
KVH = 8
HD = 64
GROUP = H // KVH
PAIR = 2 * HD
QB = 128
KB = 256

NORM_EPSILON = 1e-05
ROPE_THETA = 1000000.0
SCALE = HD**-0.5

ALL = ("y", "x", "c", "r", "z")
HEADS = ("y", "x", "c")
SPREAD = ("r", "z")
TOKS = ("y", "z")
HIDDEN = ("x", "c", "r")

F32 = jnp.float32
BF16 = jnp.bfloat16
VMEM_LIMIT = 60 << 20


def dot_nt(a, b):
    return lax.dot_general(a, b, (((1,), (1,)), ((), ())), preferred_element_type=F32)


def dot_nn(a, b):
    return lax.dot_general(a, b, (((1,), (0,)), ((), ())), preferred_element_type=F32)


def dot_tn(a, b):
    return lax.dot_general(a, b, (((0,), (0,)), ((), ())), preferred_element_type=F32)


def rms_forward(values, gain):
    inverse = lax.rsqrt(jnp.mean(values * values, axis=-1, keepdims=True) + NORM_EPSILON)
    return (values * inverse * gain, inverse)


def rms_backward(values, inverse, gain, upstream):
    scaled = upstream * gain
    gain_grad = jnp.sum((upstream * values * inverse).reshape(-1, values.shape[-1]), axis=0)
    values_grad = inverse * scaled - values * inverse**3 * jnp.mean(
        scaled * values, axis=-1, keepdims=True
    )
    return (values_grad, gain_grad)


def rotate(values, cosine, sine):
    half_width = values.shape[-1] // 2
    front_half = values[..., :half_width]
    back_half = values[..., half_width:]
    return jnp.concatenate(
        [front_half * cosine - back_half * sine, back_half * cosine + front_half * sine], axis=-1
    )


def doc_start_of(row_ids, doc_starts):
    return jnp.max(
        jnp.where(doc_starts[None, :] <= row_ids[:, None], doc_starts[None, :], 0), axis=1
    )


def first_key_block(doc_ref, ndoc, row):
    start = jnp.int32(0)
    for i in range(ndoc):
        d = doc_ref[i]
        start = jnp.where(d <= row, d, start)
    return start


def doc_start_rows(doc_ref, ndoc, rows):
    start = jnp.zeros(rows.shape, jnp.int32)
    for i in range(ndoc):
        d = doc_ref[i]
        start = jnp.where(d <= rows, d, start)
    return start


def prepare_keys(kv_ref, k0, k1, v0, v1, fill):
    kv = kv_ref[...]
    turned = jnp.concatenate([kv[:, HD:], kv[:, :HD]], axis=1)
    low_half = lax.broadcasted_iota(jnp.int32, kv.shape, 1) < HD
    zero = jnp.zeros_like(kv)
    other = jnp.full_like(kv, fill)
    k0[...] = jnp.where(low_half, kv, zero)
    k1[...] = jnp.where(low_half, zero, turned)
    v0[...] = jnp.where(low_half, turned, other)
    v1[...] = jnp.where(low_half, other, kv)


def attend_kernel(ndoc, stride, doc_ref, at_ref, q_ref, kv_ref, o_ref, of_ref, l_ref, k0, k1, v0, v1, even, odd):
    step = pl.program_id(0)

    @pl.when(step == 0)
    def _():
        prepare_keys(kv_ref, k0, k1, v0, v1, 1.0)

    base = (step * stride + at_ref[0]) * QB
    first = first_key_block(doc_ref, ndoc, base) // KB
    last_doc = first_key_block(doc_ref, ndoc, base + QB - 1)
    last = (base + QB - 1) // KB
    queries = jnp.concatenate([q_ref[:, :PAIR], q_ref[:, PAIR:]], axis=0)
    rows = base + lax.broadcasted_iota(jnp.int32, (QB, 1), 0)
    start = doc_start_rows(doc_ref, ndoc, rows)
    rows = jnp.concatenate([rows, rows], axis=0)
    start = jnp.concatenate([start, start], axis=0)
    even[...] = jnp.zeros_like(even)
    odd[...] = jnp.zeros_like(odd)

    def block(j, masked):
        at = pl.ds(pl.multiple_of(j * KB, KB), KB)
        for keys, values, acc in ((k0, v0, even), (k1, v1, odd)):
            p = jnp.exp(dot_nt(queries, keys[at, :]))
            if masked:
                cols = j * KB + lax.broadcasted_iota(jnp.int32, p.shape, 1)
                p = jnp.where((cols >= start) & (cols <= rows), p, 0.0)
            acc[...] += dot_nn(p.astype(BF16), values[at, :])

    def body(j, carry):
        whole = (j * KB >= last_doc) & (j * KB + KB - 1 <= base)

        @pl.when(whole)
        def _():
            block(j, False)

        @pl.when(jnp.logical_not(whole))
        def _():
            block(j, True)

        return carry

    lax.fori_loop(first, last + 1, body, 0)
    low_half = lax.broadcasted_iota(jnp.int32, even.shape, 1) < HD
    ev, od = even[...], odd[...]
    total = jnp.where(low_half, od, ev)
    total = jnp.concatenate([total[:, HD:], total[:, :HD]], axis=1)
    mixed = jnp.where(low_half, ev, od) / total
    minus_log = -jnp.log(total)
    for pair in range(2):
        part = mixed[pair * QB : (pair + 1) * QB]
        o_ref[:, pair * PAIR : (pair + 1) * PAIR] = part.astype(BF16)
        of_ref[:, pair * PAIR : (pair + 1) * PAIR] = part
        turned = jnp.transpose(minus_log[pair * QB : (pair + 1) * QB])
        l_ref[0, pair : pair + 1, :] = turned[0:1]
        l_ref[0, pair + 2 : pair + 3, :] = turned[HD : HD + 1]


def attend(doc_starts, at, q, kv, stride):
    rows, width = q.shape
    steps = rows // QB
    keys = kv.shape[0]
    ndoc = doc_starts.shape[0]
    row_block = lambda i, *_: (i, 0)
    return pl.pallas_call(
        functools.partial(attend_kernel, ndoc, stride),
        out_shape=(
            jax.ShapeDtypeStruct((rows, width), BF16),
            jax.ShapeDtypeStruct((rows, width), F32),
            jax.ShapeDtypeStruct((steps, GROUP, QB), F32),
        ),
        grid_spec=pltpu.PrefetchScalarGridSpec(
            num_scalar_prefetch=2,
            grid=(steps,),
            in_specs=[
                pl.BlockSpec((QB, width), row_block),
                pl.BlockSpec((keys, PAIR), lambda i, *_: (0, 0), pipeline_mode=pl.Buffered(1)),
            ],
            out_specs=[
                pl.BlockSpec((QB, width), row_block),
                pl.BlockSpec((QB, width), row_block),
                pl.BlockSpec((1, GROUP, QB), lambda i, *_: (i, 0, 0)),
            ],
            scratch_shapes=[pltpu.VMEM((keys, PAIR), BF16)] * 4 + [pltpu.VMEM((2 * QB, PAIR), F32)] * 2,
        ),
        compiler_params=pltpu.CompilerParams(vmem_limit_bytes=VMEM_LIMIT),
        cost_estimate=pl.CostEstimate(flops=2 * rows * 1024 * width * 2, bytes_accessed=8 << 20, transcendentals=rows * 4096),
        name="attend",
    )(doc_starts, at, q, kv)


def attend_back_kernel(
    ndoc, stride, doc_ref, at_ref, q_ref, do_ref, of_ref, l_ref, kv_ref, dq_ref, dkv_ref, k0, k1, v0, v1, dk, dv, dq
):
    step = pl.program_id(0)

    @pl.when(step == 0)
    def _():
        prepare_keys(kv_ref, k0, k1, v0, v1, 0.0)
        dk[...] = jnp.zeros_like(dk)
        dv[...] = jnp.zeros_like(dv)

    base = (step * stride + at_ref[0]) * QB
    first = first_key_block(doc_ref, ndoc, base) // KB
    last_doc = first_key_block(doc_ref, ndoc, base + QB - 1)
    last = (base + QB - 1) // KB
    queries = jnp.concatenate([q_ref[:, :PAIR], q_ref[:, PAIR:]], axis=0)
    grads = jnp.concatenate([do_ref[:, :PAIR], do_ref[:, PAIR:]], axis=0)
    low_half = lax.broadcasted_iota(jnp.int32, queries.shape, 1) < HD
    zero = jnp.zeros_like(queries)
    both_q = jnp.concatenate([jnp.where(low_half, queries, zero), jnp.where(low_half, zero, queries)], axis=0)
    both_g = jnp.concatenate([jnp.where(low_half, grads, zero), jnp.where(low_half, zero, grads)], axis=0)
    minus_log, delta = [], []
    for pair in range(2):
        at = slice(pair * PAIR, (pair + 1) * PAIR)
        product = jnp.transpose(do_ref[:, at].astype(F32) * of_ref[:, at])
        delta.append(
            (jnp.sum(product[:HD], axis=0, keepdims=True), jnp.sum(product[HD:], axis=0, keepdims=True))
        )
    minus_log = [
        jnp.concatenate([l_ref[0, 0:1, :], l_ref[0, 1:2, :]], axis=1),
        jnp.concatenate([l_ref[0, 2:3, :], l_ref[0, 3:4, :]], axis=1),
    ]
    delta = [jnp.concatenate([delta[0][half], delta[1][half]], axis=1) for half in range(2)]
    rows = base + lax.broadcasted_iota(jnp.int32, (1, QB), 1)
    start = doc_start_rows(doc_ref, ndoc, rows)
    rows = jnp.concatenate([rows, rows], axis=1)
    start = jnp.concatenate([start, start], axis=1)
    dq[...] = jnp.zeros_like(dq)

    def block(j, masked):
        at = pl.ds(pl.multiple_of(j * KB, KB), KB)
        probs, scores = [], []
        for half, keys, values in ((0, k0, v0), (1, k1, v1)):
            p = jnp.exp(dot_nt(keys[at, :], queries) + minus_log[half])
            if masked:
                cols = j * KB + lax.broadcasted_iota(jnp.int32, p.shape, 0)
                p = jnp.where((cols >= start) & (cols <= rows), p, 0.0)
            ds = (p * (dot_nt(values[at, :], grads) - delta[half])).astype(BF16)
            probs.append(p.astype(BF16))
            scores.append(ds)
        dv[at, :] += dot_nn(jnp.concatenate(probs, axis=1), both_g)
        dk[at, :] += dot_nn(jnp.concatenate(scores, axis=1), both_q)
        dq[...] += dot_tn(scores[0], k0[at, :]) + dot_tn(scores[1], k1[at, :])

    def body(j, carry):
        whole = (j * KB >= last_doc) & (j * KB + KB - 1 <= base)

        @pl.when(whole)
        def _():
            block(j, False)

        @pl.when(jnp.logical_not(whole))
        def _():
            block(j, True)

        return carry

    lax.fori_loop(first, last + 1, body, 0)
    dq_ref[:, :PAIR] = dq[:QB] * SCALE
    dq_ref[:, PAIR:] = dq[QB:] * SCALE

    @pl.when(step == pl.num_programs(0) - 1)
    def _():
        gk, gv = dk[...], dv[...]
        gk = gk + jnp.concatenate([gk[:, HD:], gk[:, :HD]], axis=1)
        gv = gv + jnp.concatenate([gv[:, HD:], gv[:, :HD]], axis=1)
        half = lax.broadcasted_iota(jnp.int32, gk.shape, 1) < HD
        dkv_ref[...] = jnp.where(half, gk, gv).astype(BF16)


def attend_back(doc_starts, at, q, do, of, logs, kv, stride):
    rows, width = q.shape
    steps = rows // QB
    keys = kv.shape[0]
    ndoc = doc_starts.shape[0]
    row_block = lambda i, *_: (i, 0)
    return pl.pallas_call(
        functools.partial(attend_back_kernel, ndoc, stride),
        out_shape=(
            jax.ShapeDtypeStruct((rows, width), F32),
            jax.ShapeDtypeStruct((keys, PAIR), BF16),
        ),
        grid_spec=pltpu.PrefetchScalarGridSpec(
            num_scalar_prefetch=2,
            grid=(steps,),
            in_specs=[
                pl.BlockSpec((QB, width), row_block),
                pl.BlockSpec((QB, width), row_block),
                pl.BlockSpec((QB, width), row_block),
                pl.BlockSpec((1, GROUP, QB), lambda i, *_: (i, 0, 0)),
                pl.BlockSpec((keys, PAIR), lambda i, *_: (0, 0), pipeline_mode=pl.Buffered(1)),
            ],
            out_specs=[
                pl.BlockSpec((QB, width), row_block),
                pl.BlockSpec((keys, PAIR), lambda i, *_: (0, 0), pipeline_mode=pl.Buffered(1)),
            ],
            scratch_shapes=[pltpu.VMEM((keys, PAIR), BF16)] * 4
            + [pltpu.VMEM((keys, PAIR), F32)] * 2
            + [pltpu.VMEM((2 * QB, PAIR), F32)],
        ),
        compiler_params=pltpu.CompilerParams(vmem_limit_bytes=VMEM_LIMIT),
        cost_estimate=pl.CostEstimate(flops=2 * rows * 1024 * width * 5, bytes_accessed=12 << 20, transcendentals=rows * 4096),
        name="attend_back",
    )(doc_starts, at, q, do, of, logs, kv)


def gather(value, axes, axis=0):
    return lax.all_gather(value, axes, axis=axis, tiled=True)


def scatter_sum(value, axes, axis=0):
    return lax.psum_scatter(value, axes, scatter_dimension=axis, tiled=True)


def on_device(
    tokens,
    doc_starts,
    attn_gain,
    qk_gains,
    q_weight,
    k_weight,
    v_weight,
    out_weight,
    ffn_gain,
    gate_weight,
    up_weight,
    down_weight,
    out_grad,
):
    spread = lax.axis_size("r") * lax.axis_size("z")
    place = lax.axis_index("r") * lax.axis_size("z") + lax.axis_index("z")
    at = jnp.reshape(place, (1,)).astype(jnp.int32)
    toks, width = tokens.shape
    heads = KVH
    rows = heads * toks
    q_rows, k_rows = q_weight.shape[0], k_weight.shape[0]

    own_gains = jnp.concatenate([attn_gain, ffn_gain, qk_gains])
    gains = gather(own_gains[None], ALL).astype(F32)
    n_gain, n_qk = attn_gain.shape[0], qk_gains.shape[0]
    attn_gain_f = gains[:, :n_gain].reshape(-1)
    ffn_gain_f = gains[:, n_gain : 2 * n_gain].reshape(-1)
    qk_gain_f = gains[:, 2 * n_gain :].reshape(-1)
    q_gain, k_gain = qk_gain_f[:HD], qk_gain_f[HD:]

    all_tokens = gather(tokens, HEADS)
    qkv_weight = gather(jnp.concatenate([q_weight, k_weight, v_weight], axis=0)[None], SPREAD)
    qkv_weight = jnp.concatenate(
        [
            qkv_weight[:, :q_rows].reshape(-1, width),
            qkv_weight[:, q_rows : q_rows + k_rows].reshape(-1, width),
            qkv_weight[:, q_rows + k_rows :].reshape(-1, width),
        ],
        axis=0,
    )
    o_weight = gather(out_weight, SPREAD)
    normed, _ = rms_forward(all_tokens.astype(F32), attn_gain_f)
    normed = normed.astype(BF16)
    qkv = dot_nt(normed, qkv_weight)
    q_width = GROUP * HD
    row_ids = (
        (jnp.arange(heads, dtype=jnp.int32)[:, None] * spread + place) * toks
        + jnp.arange(toks, dtype=jnp.int32)[None, :]
    ).reshape(-1)
    positions = (row_ids - doc_start_of(row_ids, doc_starts)).astype(F32)
    frequency = ROPE_THETA ** (-jnp.arange(HD // 2, dtype=F32) * 2.0 / HD)
    angle = positions[:, None] * frequency[None, :]
    cosine = jnp.cos(angle)[:, None, :]
    sine = jnp.sin(angle)[:, None, :]
    q_heads = qkv[:, :q_width].reshape(rows, GROUP, HD)
    k_heads = qkv[:, q_width : q_width + HD].reshape(rows, 1, HD)
    q_normed, q_inverse = rms_forward(q_heads, q_gain)
    k_normed, k_inverse = rms_forward(k_heads, k_gain)
    queries = rotate(q_normed, cosine, sine).reshape(rows, q_width).astype(BF16) * BF16(SCALE)
    keys = rotate(k_normed, cosine, sine).reshape(rows, HD).astype(BF16)
    own_kv = jnp.concatenate([keys, qkv[:, q_width + HD :].astype(BF16)], axis=1)
    kv = gather(own_kv[None], SPREAD).reshape(spread, heads, toks, PAIR)
    kv = jnp.swapaxes(kv, 0, 1).reshape(spread * rows, PAIR)
    mixed, mixed_f, logs = attend(doc_starts, at, queries, kv, spread)

    all_mixed = gather(mixed, HEADS, axis=1)
    projected = dot_nt(all_mixed, o_weight).astype(BF16)
    projected = lax.all_to_all(projected, HEADS, split_axis=0, concat_axis=1, tiled=True)
    hidden_in = tokens.astype(F32)
    hidden = hidden_in + projected.astype(F32)
    normed_two, inverse_two = rms_forward(hidden, ffn_gain_f)

    gate_rows = gather(gate_weight, HIDDEN)
    up_rows = gather(up_weight, HIDDEN)
    down_rows = gather(down_weight, HIDDEN)
    ffn_in = gather(normed_two.astype(BF16), TOKS)
    ffn_grad = gather(out_grad, TOKS)
    gate = dot_nt(ffn_in, gate_rows)
    upward = dot_nt(ffn_in, up_rows)
    sigmoid_gate = jax.nn.sigmoid(gate)
    silu_gate = gate * sigmoid_gate
    active = (silu_gate * upward).astype(BF16)
    active_grad = dot_nt(ffn_grad, down_rows)
    silu_slope = sigmoid_gate * (1.0 + gate * (1.0 - sigmoid_gate))
    gate_grad = (active_grad * upward * silu_slope).astype(BF16)
    up_grad = (active_grad * silu_gate).astype(BF16)
    ffn_in_grad = (dot_nn(gate_grad, gate_rows) + dot_nn(up_grad, up_rows)).astype(BF16)
    ffn_in_grad = scatter_sum(ffn_in_grad, TOKS).astype(F32)
    ffn_out = scatter_sum(dot_nn(active, down_rows).astype(BF16), TOKS).astype(F32)
    output = hidden + ffn_out
    gate_out = scatter_sum(dot_tn(gate_grad, ffn_in).astype(BF16), HIDDEN).astype(F32)
    up_out = scatter_sum(dot_tn(up_grad, ffn_in).astype(BF16), HIDDEN).astype(F32)
    down_out = scatter_sum(dot_tn(active, ffn_grad).astype(BF16), HIDDEN).astype(F32)

    norm_grad, ffn_gain_grad = rms_backward(hidden, inverse_two, ffn_gain_f, ffn_in_grad)
    hidden_grad = out_grad.astype(F32) + norm_grad
    hidden_low = hidden_grad.astype(BF16)
    grad_cols = lax.all_to_all(hidden_low, HEADS, split_axis=1, concat_axis=0, tiled=True)
    mixed_grad = scatter_sum(dot_nn(grad_cols, o_weight).astype(BF16), HEADS, axis=1)
    out_wgrad = dot_tn(grad_cols, all_mixed)
    o_out = scatter_sum(out_wgrad.astype(BF16), SPREAD).astype(F32)
    q_grad, kv_grad = attend_back(doc_starts, at, queries, mixed_grad, mixed_f, logs, kv, spread)
    kv_grad = jnp.swapaxes(kv_grad.reshape(heads, spread, toks, PAIR), 0, 1)
    kv_grad = scatter_sum(kv_grad.reshape(spread * rows, PAIR), SPREAD)

    q_turned = rotate(q_grad.reshape(rows, GROUP, HD), cosine, -sine)
    k_turned = rotate(kv_grad[:, :HD].astype(F32).reshape(rows, 1, HD), cosine, -sine)
    q_raw_grad, q_gain_grad = rms_backward(q_heads, q_inverse, q_gain, q_turned)
    k_raw_grad, k_gain_grad = rms_backward(k_heads, k_inverse, k_gain, k_turned)
    qkv_grad = jnp.concatenate(
        [q_raw_grad.reshape(rows, q_width), k_raw_grad.reshape(rows, HD)], axis=1
    ).astype(BF16)
    qkv_grad = jnp.concatenate([qkv_grad, kv_grad[:, HD:]], axis=1)
    normed_grad = scatter_sum(dot_nn(qkv_grad, qkv_weight).astype(BF16), HEADS).astype(F32)
    qkv_wgrad = dot_tn(qkv_grad, normed).astype(BF16)
    qkv_wgrad = jnp.concatenate(
        [
            qkv_wgrad[:q_width].reshape(spread, q_rows, width),
            qkv_wgrad[q_width : q_width + HD].reshape(spread, k_rows, width),
            qkv_wgrad[q_width + HD :].reshape(spread, k_rows, width),
        ],
        axis=1,
    )
    qkv_out = scatter_sum(qkv_wgrad, SPREAD)[0].astype(F32)
    _, inverse_one = rms_forward(hidden_in, attn_gain_f)
    input_norm_grad, attn_gain_grad = rms_backward(hidden_in, inverse_one, attn_gain_f, normed_grad)
    input_grad = hidden_grad + input_norm_grad
    members = attn_gain_grad.shape[0] // n_gain
    gain_grads = jnp.concatenate(
        [
            attn_gain_grad.reshape(members, n_gain),
            ffn_gain_grad.reshape(members, n_gain),
            jnp.concatenate([q_gain_grad, k_gain_grad]).reshape(members, n_qk),
        ],
        axis=1,
    )
    gain_out = scatter_sum(gain_grads, ALL)[0]
    return (
        output,
        input_grad,
        gain_out[:n_gain],
        gain_out[2 * n_gain :],
        qkv_out[:q_rows],
        qkv_out[q_rows : q_rows + k_rows],
        qkv_out[q_rows + k_rows :],
        o_out,
        gain_out[n_gain : 2 * n_gain],
        gate_out,
        up_out,
        down_out,
    )


def solution(mesh):
    blocks, spread = mesh.shape["blk"], mesh.shape["uly"]
    fine = Mesh(mesh.devices.reshape(2, 2, 2, blocks // 8, spread), ALL)
    by_rows, by_one = P(ALL, None), P(ALL)
    return jax.shard_map(
        on_device,
        mesh=fine,
        in_specs=(
            by_rows,
            P(),
            by_one,
            by_one,
            by_rows,
            by_rows,
            by_rows,
            by_rows,
            by_one,
            by_rows,
            by_rows,
            by_rows,
            by_rows,
        ),
        out_specs=(
            by_rows,
            by_rows,
            by_one,
            by_one,
            by_rows,
            by_rows,
            by_rows,
            by_rows,
            by_one,
            by_rows,
            by_rows,
            by_rows,
        ),
        check_vma=False,
    )
```
